32 devices in a mesh: dp: 8 (over y, x, core), tensor: 4 (over z).
Axes of the slice: x: 2, y: 2, z: 4, core: 2. Of those that a mesh axis runs over, the one named last changes fastest.
Arguments:
- block_in: float32 [4096, 1024], P(('dp', 'tensor')), may hold values from -6 to 6
- cotangent: float32 [4096, 1024], P(('dp', 'tensor')), may hold values from -6 to 6
- routes: int32 [4096, 8], P('dp'), may hold values from 0 to 15, all different within a row; in each aligned block of 512 rows (0 to 511, 512 to 1023, ...) at most 288 rows name the same one
- gate_weights: float32 [4096, 8], P('dp'), may hold values from 0.02 to 0.3
- norm_gains: float32 [2, 1024], P(None, 'dp'), may hold values from 0.5 to 1.5
- attention_weight: float32 [4, 1024, 512], P(None, 'dp', 'tensor'), may hold values from -0.1875 to 0.1875
- output_weight: float32 [2, 1024, 512], P(None, 'dp', 'tensor'), may hold values from -0.75 to 0.75
- w_gate_up: float32 [16, 2, 1024, 512], P(None, None, 'dp', 'tensor'), may hold values from -0.1875 to 0.1875
- w_down: float32 [16, 1024, 512], P(None, 'dp', 'tensor'), may hold values from -0.75 to 0.75
- m_gains: float32 [2, 1024], P(None, 'dp'), may hold values from -128 to 128
- v_gains: float32 [2, 1024], P(None, 'dp'), may hold values from 100 to 10000
- attention_first_moment: float32 [4, 1024, 512], P(None, 'dp', 'tensor'), may hold values from -12 to 12
- attention_second_moment: float32 [4, 1024, 512], P(None, 'dp', 'tensor'), may hold values from 1 to 100
- output_first_moment: float32 [2, 1024, 512], P(None, 'dp', 'tensor'), may hold values from -16 to 16
- output_second_moment: float32 [2, 1024, 512], P(None, 'dp', 'tensor'), may hold values from 1 to 100
- m_gate_up: float32 [16, 2, 1024, 512], P(None, None, 'dp', 'tensor'), may hold values from -32 to 32
- v_gate_up: float32 [16, 2, 1024, 512], P(None, None, 'dp', 'tensor'), may hold values from 10 to 1000
- m_down: float32 [16, 1024, 512], P(None, 'dp', 'tensor'), may hold values from -12 to 12
- v_down: float32 [16, 1024, 512], P(None, 'dp', 'tensor'), may hold values from 1 to 100
Outputs:
- block_out: float32 [4096, 1024], P(('dp', 'tensor'))
- input_grad: float32 [4096, 1024], P(('dp', 'tensor'))
- grad_gains: float32 [2, 1024], P(None, 'dp')
- grad_attn: float32 [4, 1024, 512], P(None, 'dp', 'tensor')
- grad_out: float32 [2, 1024, 512], P(None, 'dp', 'tensor')
- grad_gate_up: float32 [16, 2, 1024, 512], P(None, None, 'dp', 'tensor')
- grad_down: float32 [16, 1024, 512], P(None, 'dp', 'tensor')
- new_gains: float32 [2, 1024], P(None, 'dp')
- new_attn: float32 [4, 1024, 512], P(None, 'dp', 'tensor')
- new_out: float32 [2, 1024, 512], P(None, 'dp', 'tensor')
- new_gate_up: float32 [16, 2, 1024, 512], P(None, None, 'dp', 'tensor')
- new_down: float32 [16, 1024, 512], P(None, 'dp', 'tensor')
- new_m_gains: float32 [2, 1024], P(None, 'dp')
- new_v_gains: float32 [2, 1024], P(None, 'dp')
- new_m_attn: float32 [4, 1024, 512], P(None, 'dp', 'tensor')
- new_v_attn: float32 [4, 1024, 512], P(None, 'dp', 'tensor')
- new_m_out: float32 [2, 1024, 512], P(None, 'dp', 'tensor')
- new_v_out: float32 [2, 1024, 512], P(None, 'dp', 'tensor')
- new_m_gate_up: float32 [16, 2, 1024, 512], P(None, None, 'dp', 'tensor')
- new_v_gate_up: float32 [16, 2, 1024, 512], P(None, None, 'dp', 'tensor')
- new_m_down: float32 [16, 1024, 512], P(None, 'dp', 'tensor')
- new_v_down: float32 [16, 1024, 512], P(None, 'dp', 'tensor')
The draws below stay inside these ranges and needn't reach their ends.
Inputs may be any that keep to these rules, and one draw needn't show every extreme that they name: `routes`: each row names 8 different experts. Within each aligned block of 512 rows no expert is named by more than 288 rows, and in some block one expert is named by exactly 288 rows.
All inputs are finite; a program needn't handle non-finite values.
Results may differ from the reference program's by a relative error of at most 0.015.
The reference program's roundings to bfloat16 on the way count: a program that leaves them out, or rounds other values in their place, can miss the bound.
Values may be sent and summed in bfloat16 or wider, within the bound.
A program may use at most 192 MiB of HBM per device.

```python
import math
import jax
import jax.numpy as jnp
import numpy as np
from jax import lax

MODEL_WIDTH = 1024
QUERY_HEADS = 16
KEY_VALUE_HEADS = 8
HEAD_SIZE = 64
E = 16
FF = 512
TOPK = 8
SEQ = 512
SEQS = 1
STEP = 3
TOKENS = 4096
CAP = 288
N_DP = 8


def block_levels(own_key, shape, split, smallest, top_value):
    level, own = 1.0, jax.random.fold_in(own_key, 6)
    for axis_at, shards_of in split:
        heights = jnp.exp(jax.random.uniform(jax.random.fold_in(own, axis_at), (shards_of,), jnp.float32, smallest / len(split), top_value / len(split)))
        level = level * jnp.repeat(heights, shape[axis_at] // shards_of).reshape([-1 if axis == axis_at else 1 for axis in range(len(shape))])
    return level


def deal_out(own_key, own, number, rows, number_of, top, reach, slope):
    sequence = jax.random.permutation(own_key, number_of)
    heavy_load, usual = portions_of(number_of, rows * top, reach, slope, True), portions_of(number_of, rows * top, reach, slope, False)
    places = jnp.arange(number_of)

    def named(tallies, offset_by):
        used = int((tallies > 0).sum())
        fixed = max(1, used // 4)
        passed = fixed + (places - fixed + offset_by * (used - fixed)) % max(1, number_of - fixed)
        return jnp.zeros((number_of,), jnp.int32).at[sequence[jnp.where(places < fixed, places, passed)]].set(jnp.asarray(tallies, jnp.int32))

    tallies = jnp.where(number % 4 == 0, named(heavy_load, number // 4), named(usual, number - number // 4 - 1))
    mixed = jax.random.permutation(jax.random.fold_in(own, 3), number_of)
    donor, receiver = mixed[0:number_of // 2 * 2:2], mixed[1:number_of // 2 * 2:2]
    slack = jnp.minimum(tallies[donor] - 1, reach - tallies[receiver]) // 2
    slack = jnp.where((donor == sequence[0]) | (receiver == sequence[0]) | (tallies[receiver] == 0), 0, jnp.maximum(slack, 0))
    passed = jax.random.randint(jax.random.fold_in(own, 4), (number_of // 2,), 0, 1 << 20) % (slack + 1)
    tallies = tallies.at[donor].add(-passed).at[receiver].add(passed)
    items = jnp.searchsorted(jnp.cumsum(tallies), jnp.arange(rows * top), side="right").astype(jnp.int32)
    listing = items.reshape(top, rows).T
    listing = listing[jax.random.permutation(jax.random.fold_in(own, 1), rows)]
    offset_by = jax.random.randint(jax.random.fold_in(own, 2), (rows, 1), 0, top)
    return jnp.take_along_axis(listing, (jnp.arange(top)[None, :] + offset_by) % top, axis=1)


def portions_of(count, total, bound, lean, full):
    weights = [(1 << 20) // math.isqrt(rank ** lean) + 1 for rank in range(1, count + 1)]
    largest = bound if full else min(bound, max(-(-total // count), total * weights[0] // sum(weights)))
    least = 1 if total - largest >= count - 1 else 0
    counts, surplus = [largest] + [least] * (count - 1), total - largest - least * (count - 1)
    while surplus > 0:
        candidates = [i for i in range(1, count) if counts[i] < largest] or [i for i in range(1, count) if counts[i] < bound]
        pool, budget = sum([weights[i] for i in candidates]), surplus
        for i in candidates:
            addition = min(bound - counts[i], max(1, budget * weights[i] // pool), surplus)
            counts[i] = counts[i] + addition
            surplus = surplus - addition
    return np.array(counts)


def centred(own_key, shape, spread, bound, cuts=(), kind=jnp.bfloat16):
    values = jax.random.normal(own_key, shape, jnp.float32) * spread
    if len(cuts) > 0:
        values = block_levels(own_key, shape, cuts, -0.22, 0.18) * values
    return jnp.clip(values, min=-bound, max=bound).astype(kind)


def setup_inputs(seed: int = 0) -> dict:
    streams_of = jax.random.split(jax.random.key(seed), 20)
    block_in = centred(streams_of[0], (TOKENS, MODEL_WIDTH), 1.0, 6.0, ((0, 32),), jnp.float32)
    cotangent = centred(streams_of[1], (TOKENS, MODEL_WIDTH), 1.0, 6.0, ((0, 32),), jnp.float32)
    routes_keys = jax.random.split(jax.random.fold_in(streams_of[2], 1), TOKENS // (SEQS * SEQ))
    routes_turns = jax.random.permutation(jax.random.fold_in(streams_of[2], 3), TOKENS // (SEQS * SEQ))
    routes = jax.vmap(lambda own, number: deal_out(jax.random.fold_in(streams_of[2], 2), own, number, SEQS * SEQ, E, TOPK, CAP, 0))(routes_keys, routes_turns).reshape((TOKENS, TOPK))
    gate_weights = jnp.clip(0.02 + 0.28 * jax.random.uniform(streams_of[3], (TOKENS, TOPK), jnp.float32) ** block_levels(streams_of[3], (TOKENS, TOPK), ((0, 8),), -0.2, 0.2), 0.02, 0.3)
    norm_gains = jnp.clip(1.0 + 0.1 * jax.random.normal(streams_of[4], (2, MODEL_WIDTH), jnp.float32), 0.5, 1.5)
    attention_weight = centred(streams_of[5], (4, MODEL_WIDTH, KEY_VALUE_HEADS * HEAD_SIZE), MODEL_WIDTH ** -0.5, 0.1875, ((1, 8), (2, 4)), jnp.float32)
    output_weight = centred(streams_of[6], (2, MODEL_WIDTH, KEY_VALUE_HEADS * HEAD_SIZE), (QUERY_HEADS * HEAD_SIZE // 16) ** -0.5, 0.75, ((1, 8), (2, 4)), jnp.float32)
    w_gate_up = centred(streams_of[7], (E, 2, MODEL_WIDTH, FF), MODEL_WIDTH ** -0.5, 0.1875, ((2, 8), (3, 4)), jnp.float32)
    w_down = centred(streams_of[8], (E, MODEL_WIDTH, FF), (FF // 8) ** -0.5, 0.75, ((1, 8), (2, 4)), jnp.float32)
    m_gains = centred(streams_of[9], (2, MODEL_WIDTH), 20.0, 128.0, ((1, 8),), jnp.float32)
    v_gains = jnp.clip(jnp.exp(math.log(10000.0) - 4.6051702 * jax.random.uniform(streams_of[10], (2, MODEL_WIDTH), jnp.float32) ** block_levels(streams_of[10], (2, MODEL_WIDTH), ((1, 8),), -0.2, 0.2)), 100.0, 10000.0)
    attention_first_moment = centred(streams_of[11], (4, MODEL_WIDTH, KEY_VALUE_HEADS * HEAD_SIZE), 2.0, 12.0, ((1, 8), (2, 4)), jnp.float32)
    attention_second_moment = jnp.clip(jnp.exp(math.log(100.0) - 4.6051702 * jax.random.uniform(streams_of[12], (4, MODEL_WIDTH, KEY_VALUE_HEADS * HEAD_SIZE), jnp.float32) ** block_levels(streams_of[12], (4, MODEL_WIDTH, KEY_VALUE_HEADS * HEAD_SIZE), ((1, 8), (2, 4)), -0.2, 0.2)), 1.0, 100.0)
    output_first_moment = centred(streams_of[13], (2, MODEL_WIDTH, KEY_VALUE_HEADS * HEAD_SIZE), 3.0, 16.0, ((1, 8), (2, 4)), jnp.float32)
    output_second_moment = jnp.clip(jnp.exp(math.log(100.0) - 4.6051702 * jax.random.uniform(streams_of[14], (2, MODEL_WIDTH, KEY_VALUE_HEADS * HEAD_SIZE), jnp.float32) ** block_levels(streams_of[14], (2, MODEL_WIDTH, KEY_VALUE_HEADS * HEAD_SIZE), ((1, 8), (2, 4)), -0.2, 0.2)), 1.0, 100.0)
    m_gate_up = centred(streams_of[15], (E, 2, MODEL_WIDTH, FF), 5.0, 32.0, ((2, 8), (3, 4)), jnp.float32)
    v_gate_up = jnp.clip(jnp.exp(math.log(1000.0) - 4.6051702 * jax.random.uniform(streams_of[16], (E, 2, MODEL_WIDTH, FF), jnp.float32) ** block_levels(streams_of[16], (E, 2, MODEL_WIDTH, FF), ((2, 8), (3, 4)), -0.2, 0.2)), 10.0, 1000.0)
    m_down = centred(streams_of[17], (E, MODEL_WIDTH, FF), 2.0, 12.0, ((1, 8), (2, 4)), jnp.float32)
    v_down = jnp.clip(jnp.exp(math.log(100.0) - 4.6051702 * jax.random.uniform(streams_of[18], (E, MODEL_WIDTH, FF), jnp.float32) ** block_levels(streams_of[18], (E, MODEL_WIDTH, FF), ((1, 8), (2, 4)), -0.2, 0.2)), 1.0, 100.0)
    return {"block_in": block_in, "cotangent": cotangent, "routes": routes, "gate_weights": gate_weights, "norm_gains": norm_gains, "attention_weight": attention_weight, "output_weight": output_weight, "w_gate_up": w_gate_up, "w_down": w_down, "m_gains": m_gains, "v_gains": v_gains, "attention_first_moment": attention_first_moment, "attention_second_moment": attention_second_moment, "output_first_moment": output_first_moment, "output_second_moment": output_second_moment, "m_gate_up": m_gate_up, "v_gate_up": v_gate_up, "m_down": m_down, "v_down": v_down}


norm_eps = 1e-05
beta_one = 0.9
beta_two = 0.95
adam_eps = 1e-08
rate_matrix = 0.02
rate_gain = 0.2
decay_matrix = 0.1
rope_base = 10000.0

def product(form, left, right):
    return jnp.einsum(form, left.astype(jnp.float32), right.astype(jnp.float32), precision=lax.Precision.HIGHEST)

def rope_tables(length, width):
    half_width = width // 2
    frequency = rope_base ** (-(2.0 * jnp.arange(half_width, dtype=jnp.float32)) / width)
    angles = jnp.arange(length, dtype=jnp.float32)[:, None] * frequency[None, :]
    return (jnp.cos(angles)[:, None, :], jnp.sin(angles)[:, None, :])

def rotate(vectors, cos_table, sine_table):
    half_width = vectors.shape[-1] // 2
    lower_half = vectors[..., :half_width]
    upper_half = vectors[..., half_width:]
    return jnp.concatenate([lower_half * cos_table - upper_half * sine_table, upper_half * cos_table + lower_half * sine_table], axis=-1)

def unrotate(vectors, cos_table, sine_table):
    half_width = vectors.shape[-1] // 2
    lower_half = vectors[..., :half_width]
    upper_half = vectors[..., half_width:]
    return jnp.concatenate([lower_half * cos_table + upper_half * sine_table, upper_half * cos_table - lower_half * sine_table], axis=-1)

def causal_scores(queries, keys_rot):
    scale = queries.shape[-1] ** (-0.5)
    scores = product('jqgh,kgh->jgqk', queries, keys_rot) * scale
    length = scores.shape[-1]
    allowed = lax.broadcasted_iota(jnp.int32, (length, length), 0) >= lax.broadcasted_iota(jnp.int32, (length, length), 1)
    return jnp.where(allowed, scores, -jnp.inf)

def attend(items):
    queries, keys_rot, values = items
    scores = causal_scores(queries, keys_rot)
    log_totals = jax.nn.logsumexp(scores, axis=-1)
    softmax_b = jnp.exp(scores - log_totals[..., None]).astype(jnp.bfloat16)
    attended = product('jgqk,kgh->jqgh', softmax_b, values).astype(jnp.bfloat16)
    return (attended, log_totals)

def attend_back(items):
    queries, keys_rot, values, attended, log_totals, attended_cot = items
    scale = queries.shape[-1] ** (-0.5)
    scores = causal_scores(queries, keys_rot)
    softmax_f = jnp.exp(scores - log_totals[..., None])
    softmax_b = softmax_f.astype(jnp.bfloat16)
    value_cot = product('jgqk,jqgh->kgh', softmax_b, attended_cot)
    weight_cot = product('jqgh,kgh->jgqk', attended_cot, values)
    row_dots = product('jqgh,jqgh->jgq', attended_cot, attended)
    score_cot = (softmax_f * (weight_cot - row_dots[..., None])).astype(jnp.bfloat16)
    query_cot = product('jgqk,kgh->jqgh', score_cot, keys_rot) * scale
    key_cot = product('jgqk,jqgh->kgh', score_cot, queries) * scale
    return (query_cot, key_cot, value_cot)

def slot_table(route_rows, gate_rows, tok_count):
    hits = (route_rows[:, :, None] == jnp.arange(E, dtype=jnp.int32)[None, None, :]).astype(jnp.int32)
    per_token = lax.optimization_barrier(jnp.sum(hits, axis=1, dtype=jnp.int32))
    before = jnp.cumsum(per_token, axis=0, dtype=jnp.int32) - per_token
    position = lax.optimization_barrier(jnp.sum(hits * before[:, None, :], axis=2, dtype=jnp.int32))
    flat_slot = (route_rows * CAP + position).reshape(-1).astype(jnp.int32)
    owner = jnp.broadcast_to(jnp.arange(tok_count, dtype=jnp.int32)[:, None], route_rows.shape).reshape(-1)
    slot_token = jnp.full((E * CAP,), tok_count, jnp.int32).at[flat_slot].set(owner)
    slot_weight = jnp.zeros((E * CAP,), jnp.float32).at[flat_slot].set(gate_rows.reshape(-1))
    return (slot_token, slot_weight)

def group_pass(block_rows, cot_rows, route_rows, gate_rows, gains_b, attn_b, out_b, gate_up_b, down_b, cos_table, sine_table):
    tok_count = block_rows.shape[0]
    seq_count = tok_count // SEQ
    width = block_rows.shape[1]
    kv_count = attn_b.shape[2] // HEAD_SIZE
    gain_one = gains_b[0].astype(jnp.float32)
    gain_two = gains_b[1].astype(jnp.float32)
    inv_one = lax.rsqrt(lax.optimization_barrier(jnp.mean(block_rows * block_rows, axis=1, keepdims=True)) + norm_eps)
    normed_one = (block_rows * inv_one * gain_one).astype(jnp.bfloat16)
    projected = product('td,zdc->ztc', normed_one, attn_b)
    head_vals = projected.reshape(4, seq_count, SEQ, kv_count, HEAD_SIZE)
    queries = rotate(head_vals[0:2], cos_table, sine_table).astype(jnp.bfloat16).transpose(1, 0, 2, 3, 4)
    keys_rot = rotate(head_vals[2], cos_table, sine_table).astype(jnp.bfloat16)
    values = head_vals[3].astype(jnp.bfloat16)
    attended, log_totals = lax.map(attend, (queries, keys_rot, values))
    attended_flat = attended.transpose(1, 0, 2, 3, 4).reshape(2, tok_count, kv_count * HEAD_SIZE)
    residual = block_rows + product('jtc,jdc->td', attended_flat, out_b)
    inv_two = lax.rsqrt(lax.optimization_barrier(jnp.mean(residual * residual, axis=1, keepdims=True)) + norm_eps)
    normed_two = (residual * inv_two * gain_two).astype(jnp.bfloat16)
    slot_token, slot_weight = slot_table(route_rows, gate_rows, tok_count)
    padded = jnp.concatenate([normed_two, jnp.zeros((1, width), jnp.bfloat16)], axis=0)
    expert_in = padded[slot_token].reshape(E, CAP, width)
    gate_up = product('ecd,ezdf->zecf', expert_in, gate_up_b)
    gate_vals = gate_up[0]
    up_vals = gate_up[1]
    hidden = (jax.nn.silu(gate_vals) * up_vals).astype(jnp.bfloat16)
    expert_out = product('ecf,edf->ecd', hidden, down_b)
    mixture = jnp.zeros((tok_count + 1, width), jnp.float32).at[slot_token].add(expert_out.reshape(E * CAP, width) * slot_weight[:, None])
    block_out = residual + mixture[:tok_count]
    cot_pad = jnp.concatenate([cot_rows, jnp.zeros((1, width), jnp.float32)], axis=0)
    slot_cot = (slot_weight[:, None] * cot_pad[slot_token]).astype(jnp.bfloat16).reshape(E, CAP, width)
    grad_down = product('ecd,ecf->edf', slot_cot, hidden)
    hidden_cot = product('ecd,edf->ecf', slot_cot, down_b)
    sigmoid_vals = jax.nn.sigmoid(gate_vals)
    gate_cot = (hidden_cot * up_vals * sigmoid_vals * (1.0 + gate_vals * (1.0 - sigmoid_vals))).astype(jnp.bfloat16)
    up_cot = (hidden_cot * gate_vals * sigmoid_vals).astype(jnp.bfloat16)
    both_cot = jnp.stack([gate_cot, up_cot])
    grad_gate_up = product('ecd,zecf->ezdf', expert_in, both_cot)
    input_cot = product('zecf,ezdf->ecd', both_cot, gate_up_b)
    normed_two_cot = jnp.zeros((tok_count + 1, width), jnp.float32).at[slot_token].add(input_cot.reshape(E * CAP, width))[:tok_count]
    scaled_two = gain_two * normed_two_cot
    residual_cot = cot_rows + inv_two * scaled_two - residual * inv_two ** 3 * lax.optimization_barrier(jnp.mean(scaled_two * residual, axis=1, keepdims=True))
    resid_cot_b = residual_cot.astype(jnp.bfloat16)
    grad_out = product('td,jtc->jdc', resid_cot_b, attended_flat)
    attended_cot = product('td,jdc->jtc', resid_cot_b, out_b).astype(jnp.bfloat16)
    attended_cot = attended_cot.reshape(2, seq_count, SEQ, kv_count, HEAD_SIZE).transpose(1, 0, 2, 3, 4)
    query_cot, key_cot, value_cot = lax.map(attend_back, (queries, keys_rot, values, attended, log_totals, attended_cot))
    query_plain = unrotate(query_cot, cos_table, sine_table).transpose(1, 0, 2, 3, 4).reshape(2, tok_count, kv_count * HEAD_SIZE)
    key_plain = unrotate(key_cot, cos_table, sine_table).reshape(1, tok_count, kv_count * HEAD_SIZE)
    proj_cot = jnp.concatenate([query_plain, key_plain, value_cot.reshape(1, tok_count, kv_count * HEAD_SIZE)], axis=0).astype(jnp.bfloat16)
    grad_attn = product('td,ztc->zdc', normed_one, proj_cot)
    normed_one_cot = product('ztc,zdc->td', proj_cot, attn_b)
    scaled_one = gain_one * normed_one_cot
    input_grad = residual_cot + inv_one * scaled_one - block_rows * inv_one ** 3 * lax.optimization_barrier(jnp.mean(scaled_one * block_rows, axis=1, keepdims=True))
    grad_gains = jnp.stack([lax.optimization_barrier(jnp.sum(normed_one_cot * block_rows * inv_one, axis=0)), lax.optimization_barrier(jnp.sum(normed_two_cot * residual * inv_two, axis=0))])
    return (block_out, input_grad, (grad_gains, grad_attn, grad_out, grad_gate_up, grad_down))

def adamw_update(weight, moment_one, moment_two, gradient, rate, decay):
    new_one = beta_one * moment_one + (1.0 - beta_one) * gradient
    new_two = beta_two * moment_two + (1.0 - beta_two) * gradient * gradient
    corrected_one = new_one / (1.0 - beta_one ** STEP)
    corrected_two = new_two / (1.0 - beta_two ** STEP)
    new_weight = weight - rate * (corrected_one / (jnp.sqrt(corrected_two) + adam_eps) + decay * weight)
    return (new_weight, new_one, new_two)

def reference(block_in, cotangent, routes, gate_weights, norm_gains, attention_weight, output_weight, w_gate_up, w_down, m_gains, v_gains, attention_first_moment, attention_second_moment, output_first_moment, output_second_moment, m_gate_up, v_gate_up, m_down, v_down):
    masters = (norm_gains, attention_weight, output_weight, w_gate_up, w_down)
    gains_b, attn_b, out_b, gate_up_b, down_b = [weight.astype(jnp.bfloat16) for weight in masters]
    cos_table, sine_table = rope_tables(SEQ, HEAD_SIZE)
    width = block_in.shape[1]
    group_tokens = SEQS * SEQ
    pieces = (block_in.reshape(N_DP, group_tokens, width), cotangent.reshape(N_DP, group_tokens, width), routes.reshape(N_DP, group_tokens, TOPK), gate_weights.reshape(N_DP, group_tokens, TOPK))
    initial = tuple((jnp.zeros(weight.shape, jnp.float32) for weight in masters))

    def one_group(totals, items):
        block_rows, cot_rows, route_rows, gate_rows = items
        block_part, grad_part, gradients = group_pass(block_rows, cot_rows, route_rows, gate_rows, gains_b, attn_b, out_b, gate_up_b, down_b, cos_table, sine_table)
        return (tuple((total + gradient for total, gradient in zip(totals, gradients))), (block_part, grad_part))
    totals, (block_parts, grad_parts) = lax.scan(one_group, initial, pieces)
    block_out = block_parts.reshape(-1, width)
    input_grad = grad_parts.reshape(-1, width)
    grad_gains, grad_attn, grad_out, grad_gate_up, grad_down = totals
    new_gains, new_m_gains, new_v_gains = adamw_update(norm_gains, m_gains, v_gains, grad_gains, rate_gain, 0.0)
    new_attn, new_m_attn, new_v_attn = adamw_update(attention_weight, attention_first_moment, attention_second_moment, grad_attn, rate_matrix, decay_matrix)
    new_out, new_m_out, new_v_out = adamw_update(output_weight, output_first_moment, output_second_moment, grad_out, rate_matrix, decay_matrix)
    new_gate_up, new_m_gate_up, new_v_gate_up = adamw_update(w_gate_up, m_gate_up, v_gate_up, grad_gate_up, rate_matrix, decay_matrix)
    new_down, new_m_down, new_v_down = adamw_update(w_down, m_down, v_down, grad_down, rate_matrix, decay_matrix)
    return (block_out, input_grad, grad_gains, grad_attn, grad_out, grad_gate_up, grad_down, new_gains, new_attn, new_out, new_gate_up, new_down, new_m_gains, new_v_gains, new_m_attn, new_v_attn, new_m_out, new_v_out, new_m_gate_up, new_v_gate_up, new_m_down, new_v_down)
```

```python
import jax
import jax.numpy as jnp
from jax import lax
from jax.sharding import PartitionSpec as P

HEAD_SIZE = 64
SEQ = 512
STEP = 3


norm_eps = 1e-05
beta_one = 0.9
beta_two = 0.95
adam_eps = 1e-08
rate_matrix = 0.02
rate_gain = 0.2
decay_matrix = 0.1
rope_base = 10000.0


def rope_tables(length, width):
    half_width = width // 2
    frequency = rope_base ** (-(2.0 * jnp.arange(half_width, dtype=jnp.float32)) / width)
    angles = jnp.arange(length, dtype=jnp.float32)[:, None] * frequency[None, :]
    return (jnp.cos(angles)[:, None, :], jnp.sin(angles)[:, None, :])


def rotate(vectors, cos_table, sine_table):
    half_width = vectors.shape[-1] // 2
    lower_half = vectors[..., :half_width]
    upper_half = vectors[..., half_width:]
    return jnp.concatenate(
        [
            lower_half * cos_table - upper_half * sine_table,
            upper_half * cos_table + lower_half * sine_table,
        ],
        axis=-1,
    )


def unrotate(vectors, cos_table, sine_table):
    half_width = vectors.shape[-1] // 2
    lower_half = vectors[..., :half_width]
    upper_half = vectors[..., half_width:]
    return jnp.concatenate(
        [
            lower_half * cos_table + upper_half * sine_table,
            upper_half * cos_table - lower_half * sine_table,
        ],
        axis=-1,
    )


def causal_scores(queries, keys_rot):
    scale = queries.shape[-1] ** (-0.5)
    scores = (
        jnp.einsum("jqgh,kgh->jgqk", queries, keys_rot, preferred_element_type=jnp.float32) * scale
    )
    length = scores.shape[-1]
    allowed = lax.broadcasted_iota(jnp.int32, (length, length), 0) >= lax.broadcasted_iota(
        jnp.int32, (length, length), 1
    )
    return jnp.where(allowed, scores, -jnp.inf)


def attend(items):
    queries, keys_rot, values = items
    scores = causal_scores(queries, keys_rot)
    log_totals = jax.nn.logsumexp(scores, axis=-1)
    softmax_b = jnp.exp(scores - log_totals[..., None]).astype(jnp.bfloat16)
    attended = jnp.einsum(
        "jgqk,kgh->jqgh", softmax_b, values, preferred_element_type=jnp.float32
    ).astype(jnp.bfloat16)
    return (attended, log_totals)


def attend_back(items):
    queries, keys_rot, values, attended, log_totals, attended_cot = items
    scale = queries.shape[-1] ** (-0.5)
    scores = causal_scores(queries, keys_rot)
    softmax_f = jnp.exp(scores - log_totals[..., None])
    softmax_b = softmax_f.astype(jnp.bfloat16)
    value_cot = jnp.einsum(
        "jgqk,jqgh->kgh", softmax_b, attended_cot, preferred_element_type=jnp.float32
    )
    weight_cot = jnp.einsum(
        "jqgh,kgh->jgqk", attended_cot, values, preferred_element_type=jnp.float32
    )
    row_dots = jnp.einsum(
        "jqgh,jqgh->jgq", attended_cot, attended, preferred_element_type=jnp.float32
    )
    score_cot = (softmax_f * (weight_cot - row_dots[..., None])).astype(jnp.bfloat16)
    query_cot = (
        jnp.einsum("jgqk,kgh->jqgh", score_cot, keys_rot, preferred_element_type=jnp.float32)
        * scale
    )
    key_cot = (
        jnp.einsum("jgqk,jqgh->kgh", score_cot, queries, preferred_element_type=jnp.float32) * scale
    )
    return (query_cot, key_cot, value_cot)


def adamw_update(weight, moment_one, moment_two, gradient, rate, decay):
    new_one = beta_one * moment_one + (1.0 - beta_one) * gradient
    new_two = beta_two * moment_two + (1.0 - beta_two) * gradient * gradient
    corrected_one = new_one / (1.0 - beta_one**STEP)
    corrected_two = new_two / (1.0 - beta_two**STEP)
    new_weight = weight - rate * (
        corrected_one / (jnp.sqrt(corrected_two) + adam_eps) + decay * weight
    )
    return (new_weight, new_one, new_two)


def local(
    block_in,
    cotangent,
    routes,
    gate_weights,
    norm_gains,
    attention_weight,
    output_weight,
    w_gate_up,
    w_down,
    m_gains,
    v_gains,
    attention_first_moment,
    attention_second_moment,
    output_first_moment,
    output_second_moment,
    m_gate_up,
    v_gate_up,
    m_down,
    v_down,
):
    bf = jnp.bfloat16
    f32 = jnp.float32
    tok_count = routes.shape[0]
    seq_count = tok_count // SEQ
    width = block_in.shape[1]
    experts = w_gate_up.shape[0]
    rows = w_gate_up.shape[2]
    units = w_gate_up.shape[3]
    cols = attention_weight.shape[2]
    kv_count = cols // HEAD_SIZE
    gains_all = lax.all_gather(norm_gains.astype(bf), "dp", axis=1, tiled=True)
    attn_rows = jnp.concatenate([attention_weight, output_weight], axis=0)
    attn_rows = attn_rows.astype(bf).transpose(1, 0, 2).reshape(rows, 6 * cols)
    attn_all = lax.all_gather(attn_rows, "dp", axis=0, tiled=True)
    proj_all = attn_all[:, : 4 * cols]
    out_all = attn_all[:, 4 * cols :]
    gate_up_rows = w_gate_up.astype(bf).transpose(2, 1, 0, 3).reshape(rows, 2 * experts * units)
    down_rows = w_down.astype(bf).transpose(1, 0, 2).reshape(rows, experts * units)

    cos_table, sine_table = rope_tables(SEQ, HEAD_SIZE)
    gain_one = gains_all[0].astype(f32)
    gain_two = gains_all[1].astype(f32)
    inv_one = lax.rsqrt(jnp.mean(block_in * block_in, axis=1, keepdims=True) + norm_eps)
    normed_one = (block_in * inv_one * gain_one).astype(bf)
    tokens_one = lax.all_gather(normed_one, "tensor", axis=0, tiled=True)
    gate_up_all = lax.all_gather(gate_up_rows, "dp", axis=0, tiled=True)
    down_all = lax.all_gather(down_rows, "dp", axis=0, tiled=True)
    cot_all = lax.all_gather(cotangent.astype(bf), "tensor", axis=0, tiled=True)
    projected = jnp.dot(tokens_one, proj_all, preferred_element_type=f32)
    head_vals = projected.reshape(seq_count, SEQ, 4, kv_count, HEAD_SIZE).transpose(2, 0, 1, 3, 4)
    queries = (
        rotate(head_vals[0:2], cos_table, sine_table).astype(bf).transpose(1, 0, 2, 3, 4)
    )
    keys_rot = rotate(head_vals[2], cos_table, sine_table).astype(bf)
    values = head_vals[3].astype(bf)
    attended, log_totals = lax.map(attend, (queries, keys_rot, values))
    attended_flat = attended.transpose(0, 2, 1, 3, 4).reshape(tok_count, 2 * cols)
    partial_value = jnp.dot(attended_flat, out_all.T, preferred_element_type=f32).astype(bf)
    residual = block_in + lax.psum_scatter(
        partial_value, "tensor", scatter_dimension=0, tiled=True
    ).astype(f32)
    inv_two = lax.rsqrt(jnp.mean(residual * residual, axis=1, keepdims=True) + norm_eps)
    normed_two = (residual * inv_two * gain_two).astype(bf)
    tokens_two = lax.all_gather(normed_two, "tensor", axis=0, tiled=True)
    expert_ids = jnp.arange(experts, dtype=jnp.int32)[None, None, :]
    token_weight = jnp.sum(
        jnp.where(routes[:, :, None] == expert_ids, gate_weights[:, :, None], 0.0), axis=1
    )
    weight_wide = jnp.broadcast_to(
        token_weight[:, :, None], (tok_count, experts, units)
    ).reshape(tok_count, experts * units)
    half = experts * units
    gate_up = jnp.dot(tokens_two, gate_up_all, preferred_element_type=f32)
    gate_vals = gate_up[:, :half]
    up_vals = gate_up[:, half:]
    sigmoid_vals = jax.nn.sigmoid(gate_vals)
    hidden = (gate_vals * sigmoid_vals * up_vals * weight_wide).astype(bf)
    hidden_cot = jnp.dot(cot_all, down_all, preferred_element_type=f32) * weight_wide
    gate_cot = (
        hidden_cot * up_vals * sigmoid_vals * (1.0 + gate_vals * (1.0 - sigmoid_vals))
    ).astype(bf)
    up_cot = (hidden_cot * gate_vals * sigmoid_vals).astype(bf)
    both_cot = jnp.concatenate([gate_cot, up_cot], axis=1)
    back_sum = lax.dot_general(
        both_cot, gate_up_all, (((1,), (1,)), ((), ())), preferred_element_type=f32
    ).astype(bf)
    normed_two_cot = lax.psum_scatter(
        back_sum, "tensor", scatter_dimension=0, tiled=True
    ).astype(f32)
    down_local = lax.dot_general(
        cot_all, hidden, (((0,), (0,)), ((), ())), preferred_element_type=f32
    ).astype(bf)
    gate_up_local = lax.dot_general(
        tokens_two, both_cot, (((0,), (0,)), ((), ())), preferred_element_type=f32
    ).astype(bf)
    mixture = lax.dot_general(
        hidden, down_all, (((1,), (1,)), ((), ())), preferred_element_type=f32
    ).astype(bf)
    block_out = residual + lax.psum_scatter(
        mixture, "tensor", scatter_dimension=0, tiled=True
    ).astype(f32)
    grad_down = lax.psum_scatter(down_local, "dp", scatter_dimension=0, tiled=True)
    grad_down = grad_down.astype(f32).reshape(rows, experts, units).transpose(1, 0, 2)
    grad_gate_up = lax.psum_scatter(gate_up_local, "dp", scatter_dimension=0, tiled=True)
    grad_gate_up = (
        grad_gate_up.astype(f32).reshape(rows, 2, experts, units).transpose(2, 1, 0, 3)
    )
    scaled_two = gain_two * normed_two_cot
    residual_cot = (
        cotangent
        + inv_two * scaled_two
        - residual * inv_two**3 * jnp.mean(scaled_two * residual, axis=1, keepdims=True)
    )
    resid_all = lax.all_gather(residual_cot.astype(bf), "tensor", axis=0, tiled=True)
    out_local = lax.dot_general(
        resid_all, attended_flat, (((0,), (0,)), ((), ())), preferred_element_type=f32
    )
    attended_cot = jnp.dot(resid_all, out_all, preferred_element_type=f32).astype(bf)
    attended_cot = attended_cot.reshape(seq_count, SEQ, 2, kv_count, HEAD_SIZE).transpose(
        0, 2, 1, 3, 4
    )
    query_cot, key_cot, value_cot = lax.map(
        attend_back, (queries, keys_rot, values, attended, log_totals, attended_cot)
    )
    query_plain = unrotate(query_cot, cos_table, sine_table)
    key_plain = unrotate(key_cot, cos_table, sine_table)
    proj_cot = jnp.concatenate(
        [
            query_plain[:, 0].reshape(tok_count, cols),
            query_plain[:, 1].reshape(tok_count, cols),
            key_plain.reshape(tok_count, cols),
            value_cot.reshape(tok_count, cols),
        ],
        axis=1,
    ).astype(bf)
    attn_local = lax.dot_general(
        tokens_one, proj_cot, (((0,), (0,)), ((), ())), preferred_element_type=f32
    )
    norm_terms = lax.dot_general(
        proj_cot, proj_all, (((1,), (1,)), ((), ())), preferred_element_type=f32
    )
    normed_one_cot = lax.psum_scatter(
        norm_terms.astype(bf), "tensor", scatter_dimension=0, tiled=True
    ).astype(f32)
    both_local = jnp.concatenate([attn_local, out_local], axis=1).astype(bf)
    both_sum = lax.psum_scatter(both_local, "dp", scatter_dimension=0, tiled=True).astype(f32)
    both_sum = both_sum.reshape(rows, 6, cols).transpose(1, 0, 2)
    grad_attn = both_sum[:4]
    grad_out = both_sum[4:]
    scaled_one = gain_one * normed_one_cot
    input_grad = (
        residual_cot
        + inv_one * scaled_one
        - block_in * inv_one**3 * jnp.mean(scaled_one * block_in, axis=1, keepdims=True)
    )
    gain_local = jnp.stack(
        [
            jnp.sum(normed_one_cot * block_in * inv_one, axis=0),
            jnp.sum(normed_two_cot * residual * inv_two, axis=0),
        ]
    )
    gain_sum = lax.psum(gain_local, ("dp", "tensor"))
    grad_gains = lax.dynamic_slice_in_dim(gain_sum, lax.axis_index("dp") * rows, rows, axis=1)
    new_gains, new_m_gains, new_v_gains = adamw_update(
        norm_gains, m_gains, v_gains, grad_gains, rate_gain, 0.0
    )
    new_attn, new_m_attn, new_v_attn = adamw_update(
        attention_weight,
        attention_first_moment,
        attention_second_moment,
        grad_attn,
        rate_matrix,
        decay_matrix,
    )
    new_out, new_m_out, new_v_out = adamw_update(
        output_weight,
        output_first_moment,
        output_second_moment,
        grad_out,
        rate_matrix,
        decay_matrix,
    )
    new_gate_up, new_m_gate_up, new_v_gate_up = adamw_update(
        w_gate_up, m_gate_up, v_gate_up, grad_gate_up, rate_matrix, decay_matrix
    )
    new_down, new_m_down, new_v_down = adamw_update(
        w_down, m_down, v_down, grad_down, rate_matrix, decay_matrix
    )
    return (
        block_out,
        input_grad,
        grad_gains,
        grad_attn,
        grad_out,
        grad_gate_up,
        grad_down,
        new_gains,
        new_attn,
        new_out,
        new_gate_up,
        new_down,
        new_m_gains,
        new_v_gains,
        new_m_attn,
        new_v_attn,
        new_m_out,
        new_v_out,
        new_m_gate_up,
        new_v_gate_up,
        new_m_down,
        new_v_down,
    )


def solution(mesh):
    return jax.shard_map(
        local,
        mesh=mesh,
        in_specs=(
            P(("dp", "tensor"), None),
            P(("dp", "tensor"), None),
            P("dp", None),
            P("dp", None),
            P(None, "dp"),
            P(None, "dp", "tensor"),
            P(None, "dp", "tensor"),
            P(None, None, "dp", "tensor"),
            P(None, "dp", "tensor"),
            P(None, "dp"),
            P(None, "dp"),
            P(None, "dp", "tensor"),
            P(None, "dp", "tensor"),
            P(None, "dp", "tensor"),
            P(None, "dp", "tensor"),
            P(None, None, "dp", "tensor"),
            P(None, None, "dp", "tensor"),
            P(None, "dp", "tensor"),
            P(None, "dp", "tensor"),
        ),
        out_specs=(
            P(("dp", "tensor"), None),
            P(("dp", "tensor"), None),
            P(None, "dp"),
            P(None, "dp", "tensor"),
            P(None, "dp", "tensor"),
            P(None, None, "dp", "tensor"),
            P(None, "dp", "tensor"),
            P(None, "dp"),
            P(None, "dp", "tensor"),
            P(None, "dp", "tensor"),
            P(None, None, "dp", "tensor"),
            P(None, "dp", "tensor"),
            P(None, "dp"),
            P(None, "dp"),
            P(None, "dp", "tensor"),
            P(None, "dp", "tensor"),
            P(None, "dp", "tensor"),
            P(None, "dp", "tensor"),
            P(None, None, "dp", "tensor"),
            P(None, None, "dp", "tensor"),
            P(None, "dp", "tensor"),
            P(None, "dp", "tensor"),
        ),
        check_vma=False,
    )
```

```python
import jax
import jax.numpy as jnp
from jax import lax
from jax.sharding import PartitionSpec as P


HEAD_SIZE = 64
SEQ = 512
STEP = 3


norm_eps = 1e-05
beta_one = 0.9
beta_two = 0.95
adam_eps = 1e-08
rate_matrix = 0.02
rate_gain = 0.2
decay_matrix = 0.1
rope_base = 10000.0


def rope_tables(length, width):
    half_width = width // 2
    frequency = rope_base ** (-(2.0 * jnp.arange(half_width, dtype=jnp.float32)) / width)
    angles = jnp.arange(length, dtype=jnp.float32)[:, None] * frequency[None, :]
    return (jnp.cos(angles)[:, None, :], jnp.sin(angles)[:, None, :])


def rotate(vectors, cos_table, sine_table):
    half_width = vectors.shape[-1] // 2
    lower_half = vectors[..., :half_width]
    upper_half = vectors[..., half_width:]
    return jnp.concatenate(
        [
            lower_half * cos_table - upper_half * sine_table,
            upper_half * cos_table + lower_half * sine_table,
        ],
        axis=-1,
    )


def unrotate(vectors, cos_table, sine_table):
    half_width = vectors.shape[-1] // 2
    lower_half = vectors[..., :half_width]
    upper_half = vectors[..., half_width:]
    return jnp.concatenate(
        [
            lower_half * cos_table + upper_half * sine_table,
            upper_half * cos_table - lower_half * sine_table,
        ],
        axis=-1,
    )


def causal_scores(queries, keys_rot):
    scale = queries.shape[-1] ** (-0.5)
    scores = (
        jnp.einsum("jqgh,kgh->jgqk", queries, keys_rot, preferred_element_type=jnp.float32) * scale
    )
    length = scores.shape[-1]
    allowed = lax.broadcasted_iota(jnp.int32, (length, length), 0) >= lax.broadcasted_iota(
        jnp.int32, (length, length), 1
    )
    return jnp.where(allowed, scores, -jnp.inf)


def attend(items):
    queries, keys_rot, values = items
    scores = causal_scores(queries, keys_rot)
    log_totals = jax.nn.logsumexp(scores, axis=-1)
    softmax_b = jnp.exp(scores - log_totals[..., None]).astype(jnp.bfloat16)
    attended = jnp.einsum(
        "jgqk,kgh->jqgh", softmax_b, values, preferred_element_type=jnp.float32
    ).astype(jnp.bfloat16)
    return (attended, log_totals)


def attend_back(items):
    queries, keys_rot, values, attended, log_totals, attended_cot = items
    scale = queries.shape[-1] ** (-0.5)
    scores = causal_scores(queries, keys_rot)
    softmax_f = jnp.exp(scores - log_totals[..., None])
    softmax_b = softmax_f.astype(jnp.bfloat16)
    value_cot = jnp.einsum(
        "jgqk,jqgh->kgh", softmax_b, attended_cot, preferred_element_type=jnp.float32
    )
    weight_cot = jnp.einsum(
        "jqgh,kgh->jgqk", attended_cot, values, preferred_element_type=jnp.float32
    )
    row_dots = jnp.einsum(
        "jqgh,jqgh->jgq", attended_cot, attended, preferred_element_type=jnp.float32
    )
    score_cot = (softmax_f * (weight_cot - row_dots[..., None])).astype(jnp.bfloat16)
    query_cot = (
        jnp.einsum("jgqk,kgh->jqgh", score_cot, keys_rot, preferred_element_type=jnp.float32)
        * scale
    )
    key_cot = (
        jnp.einsum("jgqk,jqgh->kgh", score_cot, queries, preferred_element_type=jnp.float32) * scale
    )
    return (query_cot, key_cot, value_cot)


def adamw_update(weight, moment_one, moment_two, gradient, rate, decay):
    new_one = beta_one * moment_one + (1.0 - beta_one) * gradient
    new_two = beta_two * moment_two + (1.0 - beta_two) * gradient * gradient
    corrected_one = new_one / (1.0 - beta_one**STEP)
    corrected_two = new_two / (1.0 - beta_two**STEP)
    new_weight = weight - rate * (
        corrected_one / (jnp.sqrt(corrected_two) + adam_eps) + decay * weight
    )
    return (new_weight, new_one, new_two)


def gather_tokens(block):
    count = lax.axis_size("tensor")
    me = lax.axis_index("tensor")
    rows = block.shape[0]
    whole = jnp.zeros((count * rows, block.shape[1]), block.dtype)
    whole = lax.dynamic_update_slice_in_dim(whole, block, me * rows, axis=0)
    arrived = []
    for shift in range(1, count):
        ring = [(i, (i + shift) % count) for i in range(count)]
        arrived.append(lax.ppermute(block, "tensor", ring))
    for shift in range(1, count):
        source = (me + count - shift) % count
        whole = lax.dynamic_update_slice_in_dim(whole, arrived[shift - 1], source * rows, axis=0)
    return whole


def scatter_tokens(partial):
    count = lax.axis_size("tensor")
    me = lax.axis_index("tensor")
    rows = partial.shape[0] // count
    sent = partial.astype(jnp.bfloat16)
    arrived = []
    for shift in range(1, count):
        ring = [(i, (i + shift) % count) for i in range(count)]
        target = (me + shift) % count
        piece = lax.dynamic_slice_in_dim(sent, target * rows, rows, axis=0)
        arrived.append(lax.ppermute(piece, "tensor", ring))
    total = lax.dynamic_slice_in_dim(sent, me * rows, rows, axis=0).astype(jnp.float32)
    for piece in arrived:
        total = total + piece.astype(jnp.float32)
    return total


def local(
    block_in,
    cotangent,
    routes,
    gate_weights,
    norm_gains,
    attention_weight,
    output_weight,
    w_gate_up,
    w_down,
    m_gains,
    v_gains,
    attention_first_moment,
    attention_second_moment,
    output_first_moment,
    output_second_moment,
    m_gate_up,
    v_gate_up,
    m_down,
    v_down,
):
    bf = jnp.bfloat16
    f32 = jnp.float32
    tok_count = routes.shape[0]
    seq_count = tok_count // SEQ
    width = block_in.shape[1]
    experts = w_gate_up.shape[0]
    rows = w_gate_up.shape[2]
    units = w_gate_up.shape[3]
    cols = attention_weight.shape[2]
    kv_count = cols // HEAD_SIZE
    gains_all = lax.all_gather(norm_gains.astype(bf), "dp", axis=1, tiled=True)
    attn_rows = jnp.concatenate([attention_weight, output_weight], axis=0)
    attn_rows = attn_rows.astype(bf).transpose(1, 0, 2).reshape(rows, 6 * cols)
    attn_all = lax.all_gather(attn_rows, "dp", axis=0, tiled=True)
    proj_all = attn_all[:, : 4 * cols]
    out_all = attn_all[:, 4 * cols :]
    gate_up_rows = w_gate_up.astype(bf).transpose(2, 1, 0, 3).reshape(rows, 2 * experts * units)
    down_rows = w_down.astype(bf).transpose(1, 0, 2).reshape(rows, experts * units)

    cos_table, sine_table = rope_tables(SEQ, HEAD_SIZE)
    gain_one = gains_all[0].astype(f32)
    gain_two = gains_all[1].astype(f32)
    inv_one = lax.rsqrt(jnp.mean(block_in * block_in, axis=1, keepdims=True) + norm_eps)
    normed_one = (block_in * inv_one * gain_one).astype(bf)
    tokens_one = gather_tokens(normed_one)
    half = experts * units
    expert_rows = jnp.concatenate([gate_up_rows, down_rows], axis=1)
    expert_all = lax.all_gather(expert_rows, "dp", axis=0, tiled=True)
    gate_up_all = expert_all[:, : 2 * half]
    down_all = expert_all[:, 2 * half :]
    cot_rows, tokens_one = lax.optimization_barrier((cotangent.astype(bf), tokens_one))
    cot_all = gather_tokens(cot_rows)
    projected = jnp.dot(tokens_one, proj_all, preferred_element_type=f32)
    head_vals = projected.reshape(seq_count, SEQ, 4, kv_count, HEAD_SIZE).transpose(2, 0, 1, 3, 4)
    queries = (
        rotate(head_vals[0:2], cos_table, sine_table).astype(bf).transpose(1, 0, 2, 3, 4)
    )
    keys_rot = rotate(head_vals[2], cos_table, sine_table).astype(bf)
    values = head_vals[3].astype(bf)
    attended, log_totals = lax.map(attend, (queries, keys_rot, values))
    attended_flat = attended.transpose(0, 2, 1, 3, 4).reshape(tok_count, 2 * cols)
    partial_value = jnp.dot(attended_flat, out_all.T, preferred_element_type=f32).astype(bf)
    partial_value, cot_all = lax.optimization_barrier((partial_value, cot_all))
    residual = block_in + scatter_tokens(partial_value)
    inv_two = lax.rsqrt(jnp.mean(residual * residual, axis=1, keepdims=True) + norm_eps)
    normed_two = (residual * inv_two * gain_two).astype(bf)
    tokens_two = gather_tokens(normed_two)
    expert_ids = jnp.arange(experts, dtype=jnp.int32)[None, None, :]
    token_weight = jnp.sum(
        jnp.where(routes[:, :, None] == expert_ids, gate_weights[:, :, None], 0.0), axis=1
    )
    weight_wide = jnp.broadcast_to(
        token_weight[:, :, None], (tok_count, experts, units)
    ).reshape(tok_count, experts * units)
    gate_up = jnp.dot(tokens_two, gate_up_all, preferred_element_type=f32)
    gate_vals = gate_up[:, :half]
    up_vals = gate_up[:, half:]
    sigmoid_vals = jax.nn.sigmoid(gate_vals)
    hidden = (gate_vals * sigmoid_vals * up_vals * weight_wide).astype(bf)
    hidden_cot = jnp.dot(cot_all, down_all, preferred_element_type=f32) * weight_wide
    gate_cot = (
        hidden_cot * up_vals * sigmoid_vals * (1.0 + gate_vals * (1.0 - sigmoid_vals))
    ).astype(bf)
    up_cot = (hidden_cot * gate_vals * sigmoid_vals).astype(bf)
    both_cot = jnp.concatenate([gate_cot, up_cot], axis=1)
    back_sum = lax.dot_general(
        both_cot, gate_up_all, (((1,), (1,)), ((), ())), preferred_element_type=f32
    ).astype(bf)
    normed_two_cot = scatter_tokens(back_sum)
    down_local = lax.dot_general(
        cot_all, hidden, (((0,), (0,)), ((), ())), preferred_element_type=f32
    ).astype(bf)
    gate_up_local = lax.dot_general(
        tokens_two, both_cot, (((0,), (0,)), ((), ())), preferred_element_type=f32
    ).astype(bf)
    expert_local = jnp.concatenate([gate_up_local, down_local], axis=1)
    scaled_two = gain_two * normed_two_cot
    residual_cot = (
        cotangent
        + inv_two * scaled_two
        - residual * inv_two**3 * jnp.mean(scaled_two * residual, axis=1, keepdims=True)
    )
    resid_rows, expert_local = lax.optimization_barrier((residual_cot.astype(bf), expert_local))
    expert_sum = lax.psum_scatter(expert_local, "dp", scatter_dimension=0, tiled=True).astype(f32)
    resid_all = gather_tokens(resid_rows)
    hidden, resid_all = lax.optimization_barrier((hidden, resid_all))
    mixture = lax.dot_general(
        hidden, down_all, (((1,), (1,)), ((), ())), preferred_element_type=f32
    ).astype(bf)
    block_out = residual + scatter_tokens(mixture)
    out_local = lax.dot_general(
        resid_all, attended_flat, (((0,), (0,)), ((), ())), preferred_element_type=f32
    )
    attended_cot = jnp.dot(resid_all, out_all, preferred_element_type=f32).astype(bf)
    attended_cot = attended_cot.reshape(seq_count, SEQ, 2, kv_count, HEAD_SIZE).transpose(
        0, 2, 1, 3, 4
    )
    query_cot, key_cot, value_cot = lax.map(
        attend_back, (queries, keys_rot, values, attended, log_totals, attended_cot)
    )
    query_plain = unrotate(query_cot, cos_table, sine_table)
    key_plain = unrotate(key_cot, cos_table, sine_table)
    proj_cot = jnp.concatenate(
        [
            query_plain[:, 0].reshape(tok_count, cols),
            query_plain[:, 1].reshape(tok_count, cols),
            key_plain.reshape(tok_count, cols),
            value_cot.reshape(tok_count, cols),
        ],
        axis=1,
    ).astype(bf)
    attn_local = lax.dot_general(
        tokens_one, proj_cot, (((0,), (0,)), ((), ())), preferred_element_type=f32
    )
    norm_terms = lax.dot_general(
        proj_cot, proj_all, (((1,), (1,)), ((), ())), preferred_element_type=f32
    )
    normed_one_cot = scatter_tokens(norm_terms.astype(bf))
    both_local = jnp.concatenate([attn_local, out_local], axis=1).astype(bf)
    both_local, expert_sum = lax.optimization_barrier((both_local, expert_sum))
    both_sum = lax.psum_scatter(both_local, "dp", scatter_dimension=0, tiled=True).astype(f32)
    both_sum = both_sum.reshape(rows, 6, cols).transpose(1, 0, 2)
    grad_down = expert_sum[:, 2 * half :].reshape(rows, experts, units).transpose(1, 0, 2)
    grad_gate_up = (
        expert_sum[:, : 2 * half].reshape(rows, 2, experts, units).transpose(2, 1, 0, 3)
    )
    grad_attn = both_sum[:4]
    grad_out = both_sum[4:]
    scaled_one = gain_one * normed_one_cot
    input_grad = (
        residual_cot
        + inv_one * scaled_one
        - block_in * inv_one**3 * jnp.mean(scaled_one * block_in, axis=1, keepdims=True)
    )
    gain_local = jnp.stack(
        [
            jnp.sum(normed_one_cot * block_in * inv_one, axis=0),
            jnp.sum(normed_two_cot * residual * inv_two, axis=0),
        ]
    )
    gain_sum = lax.psum(gain_local, ("dp", "tensor"))
    grad_gains = lax.dynamic_slice_in_dim(gain_sum, lax.axis_index("dp") * rows, rows, axis=1)
    new_gains, new_m_gains, new_v_gains = adamw_update(
        norm_gains, m_gains, v_gains, grad_gains, rate_gain, 0.0
    )
    new_attn, new_m_attn, new_v_attn = adamw_update(
        attention_weight,
        attention_first_moment,
        attention_second_moment,
        grad_attn,
        rate_matrix,
        decay_matrix,
    )
    new_out, new_m_out, new_v_out = adamw_update(
        output_weight,
        output_first_moment,
        output_second_moment,
        grad_out,
        rate_matrix,
        decay_matrix,
    )
    new_gate_up, new_m_gate_up, new_v_gate_up = adamw_update(
        w_gate_up, m_gate_up, v_gate_up, grad_gate_up, rate_matrix, decay_matrix
    )
    new_down, new_m_down, new_v_down = adamw_update(
        w_down, m_down, v_down, grad_down, rate_matrix, decay_matrix
    )
    return (
        block_out,
        input_grad,
        grad_gains,
        grad_attn,
        grad_out,
        grad_gate_up,
        grad_down,
        new_gains,
        new_attn,
        new_out,
        new_gate_up,
        new_down,
        new_m_gains,
        new_v_gains,
        new_m_attn,
        new_v_attn,
        new_m_out,
        new_v_out,
        new_m_gate_up,
        new_v_gate_up,
        new_m_down,
        new_v_down,
    )


def solution(mesh):
    return jax.shard_map(
        local,
        mesh=mesh,
        in_specs=(
            P(("dp", "tensor"), None),
            P(("dp", "tensor"), None),
            P("dp", None),
            P("dp", None),
            P(None, "dp"),
            P(None, "dp", "tensor"),
            P(None, "dp", "tensor"),
            P(None, None, "dp", "tensor"),
            P(None, "dp", "tensor"),
            P(None, "dp"),
            P(None, "dp"),
            P(None, "dp", "tensor"),
            P(None, "dp", "tensor"),
            P(None, "dp", "tensor"),
            P(None, "dp", "tensor"),
            P(None, None, "dp", "tensor"),
            P(None, None, "dp", "tensor"),
            P(None, "dp", "tensor"),
            P(None, "dp", "tensor"),
        ),
        out_specs=(
            P(("dp", "tensor"), None),
            P(("dp", "tensor"), None),
            P(None, "dp"),
            P(None, "dp", "tensor"),
            P(None, "dp", "tensor"),
            P(None, None, "dp", "tensor"),
            P(None, "dp", "tensor"),
            P(None, "dp"),
            P(None, "dp", "tensor"),
            P(None, "dp", "tensor"),
            P(None, None, "dp", "tensor"),
            P(None, "dp", "tensor"),
            P(None, "dp"),
            P(None, "dp"),
            P(None, "dp", "tensor"),
            P(None, "dp", "tensor"),
            P(None, "dp", "tensor"),
            P(None, "dp", "tensor"),
            P(None, None, "dp", "tensor"),
            P(None, None, "dp", "tensor"),
            P(None, "dp", "tensor"),
            P(None, "dp", "tensor"),
        ),
        check_vma=False,
    )
```
